512 devices in a mesh: bulk: 32 (over z, core), blk: 16 (over y, x).
Axes of the slice: x: 4, y: 4, z: 16, core: 2. Of those that a mesh axis runs over, the one named last changes fastest.
Arguments:
- factor: float32 [131072, 4096], P(('bulk', 'blk')), parts along dimension 0, as said below
- initial: float32 [131072, 128], P(('bulk', 'blk')), parts along dimension 0, may hold values from -6 to 6
- bounds: float32 [64], P('bulk'), parts along dimension 0, may hold values from 0 to 15.5, as said below
Outputs:
- basis_rows: float32 [131072, 128], P(('bulk', 'blk')), parts along dimension 0
- projected: float32 [4096, 128], P('bulk'), parts along dimension 0
- residual: float32 [131072, 128], P(('bulk', 'blk')), parts along dimension 0
The draws below stay inside these ranges and needn't reach their ends.
There are 32 independent parts, one for each index of `bulk`. The reference program is written for one: setup_inputs(seed, part) draws one part's arguments, and reference() takes and returns one part's arrays. A program takes and returns all parts, laid end to end along the dimension named above; each array names one. Nothing has to cross between parts.
Inputs may be any that keep to these rules, and one draw needn't show every extreme that they name: factor is symmetric. `bounds`: the upper end exceeds the lower end by 14 or more.
All inputs are finite; a program needn't handle non-finite values.
Results may differ from the reference program's by a relative error of at most 0.0003.
Values sent between devices are 32-bit elements; how exact they have to be, the bound alone decides.
A program may use at most 64 MiB of HBM per device.

```python
import jax
import jax.numpy as jnp
from jax import lax

N = 4096
K = 128
DEGREE = 8


def draw_factor(key, part):
    first_key = jax.random.fold_in(key, 11)
    second_key = jax.random.fold_in(key, 12)
    entries = jax.random.normal(first_key, (N, N), jnp.float32)
    symmetric_part = (entries + entries.T) * (0.70710678 * 1.6 / jnp.sqrt(jnp.float32(N)))
    diagonal = jnp.exp(jax.random.uniform(second_key, (N,), jnp.float32, jnp.log(4.0), jnp.log(11.0)))
    return symmetric_part + jnp.diag(diagonal)


def draw_bounds(key, part):
    low_key = jax.random.fold_in(key, 21)
    high_key = jax.random.fold_in(key, 22)
    low_end = jax.random.uniform(low_key, (1,), jnp.float32, 0.0, 0.5)
    high_end = jax.random.uniform(high_key, (1,), jnp.float32, 14.8, 15.3)
    return jnp.concatenate([low_end, high_end])


def shard_levels(stream_key, extent, shards, low, largest):
    gain, own = 1.0, jax.random.fold_in(stream_key, 6)
    for axis_at, parts in shards:
        heights = jnp.exp(jax.random.uniform(jax.random.fold_in(own, axis_at), (parts,), jnp.float32, low / len(shards), largest / len(shards)))
        gain = gain * jnp.repeat(heights, extent[axis_at] // parts).reshape([-1 if axis == axis_at else 1 for axis in range(len(extent))])
    return gain


def normal_values(own_key, shape, deviation, reach, split=(), held_as=jnp.bfloat16):
    drawn = deviation * jax.random.normal(own_key, shape, jnp.float32)
    if split:
        drawn = drawn * shard_levels(own_key, shape, split, -0.22, 0.18)
    return jnp.clip(drawn, -reach, reach).astype(held_as)


def setup_inputs(seed: int = 0, part: int = 0) -> dict:
    key_list = jax.random.split(jax.random.key(seed), 4)
    part_keys = jax.random.split(jax.random.fold_in(key_list[3], part), 4)
    factor = draw_factor(jax.random.fold_in(jax.random.fold_in(key_list[3], part), 71), part)
    initial = normal_values(part_keys[1], (N, K), 1.0, 6.0, ((0, 16),), jnp.float32)
    bounds = draw_bounds(jax.random.fold_in(jax.random.fold_in(key_list[3], part), 71), part)
    return dict(factor=factor, initial=initial, bounds=bounds)


def product(factor, vectors):
    return jnp.dot(factor.astype(jnp.float32), vectors.astype(jnp.float32), precision=lax.Precision.HIGHEST, preferred_element_type=jnp.float32)

def lower_solve(cholesky_low, right_side):
    return lax.linalg.triangular_solve(cholesky_low, right_side, left_side=True, lower=True)

def reference(factor, initial, bounds):
    centre = (bounds[0] + bounds[1]) / 2.0
    radius = (bounds[1] - bounds[0]) / 2.0
    previous = initial
    current = (product(factor, initial) - centre * initial) / radius
    for order_step in range(DEGREE - 1):
        scaled = (product(factor, current) - centre * current) / radius
        following = 2.0 * scaled - previous
        previous = current
        current = following
    filtered = current
    gram_matrix = jnp.dot(filtered.T.astype(jnp.float32), filtered.astype(jnp.float32), precision=lax.Precision.HIGHEST, preferred_element_type=jnp.float32)
    cholesky_low = jnp.linalg.cholesky(gram_matrix)
    basis_rows = lower_solve(cholesky_low, filtered.T).T
    mapped = product(factor, basis_rows)
    projected = jnp.dot(basis_rows.T.astype(jnp.float32), mapped.astype(jnp.float32), precision=lax.Precision.HIGHEST, preferred_element_type=jnp.float32)
    residual = mapped - jnp.dot(basis_rows.astype(jnp.float32), projected.astype(jnp.float32), precision=lax.Precision.HIGHEST, preferred_element_type=jnp.float32)
    return (basis_rows, projected, residual)
```

```python
import functools

import jax
import jax.numpy as jnp
from jax import lax
from jax.experimental import pallas as pl
from jax.experimental.pallas import tpu as pltpu
from jax.sharding import PartitionSpec as P

DEGREE = 8
SIDE = 4
CHAINS = 4
PANEL = 32
X, Y = 0, 1
FIRST = (X, Y, X, Y)
MESH = pl.DeviceIdType.MESH
F32, BF16 = jnp.float32, jnp.bfloat16
HIGHEST = lax.Precision.HIGHEST
NN = (((1,), (0,)), ((), ()))
NT = (((1,), (1,)), ((), ()))
TN = (((0,), (0,)), ((), ()))

OVER_X = ((1, 1), (3, 3), (2, 1), (2, 3))
OVER_Y = ((1, 3), (3, 1), (1, 2), (3, 2))


def exact_dot(left, right, dims):
    return lax.dot_general(left, right, dims, precision=HIGHEST, preferred_element_type=F32)


def xor(value, k):
    if k == 0:
        return value
    if k == 1:
        return value + 1 - 2 * (value % 2)
    if k == 2:
        return (value + 2) % 4
    return 3 - value


def split(value):
    high = value.astype(BF16)
    low = (value - high.astype(F32)).astype(BF16)
    return high, low


def kernel(
    factor, initial, bounds,
    basis_out, projected_out, residual_out,
    own_rows, arrived, arrived_half, w_high, w_low, vectors, stacked, partial_own, partial_out, partial_in, gathered,
    small_out, small_in, work,
    own_sem, block_send, block_recv, rs_send, rs_recv, ag_send, ag_recv, small_send, small_recv,
):
    me = lax.axis_index("blk")
    my_y, my_x = me // SIDE, me % SIDE
    nb = own_rows.shape[0]
    kc = partial_own.shape[1]
    k_all = CHAINS * kc

    def peer(axis, k):
        if axis == X:
            return {"blk": my_y * SIDE + xor(my_x, k)}
        return {"blk": xor(my_y, k) * SIDE + my_x}

    def column(ky, kx):
        return pl.multiple_of((xor(my_y, ky) * SIDE + xor(my_x, kx)) * nb, nb)

    def remote(src, dst, send, recv, axis, k):
        return pltpu.make_async_remote_copy(
            src_ref=src, dst_ref=dst, send_sem=send, recv_sem=recv, device_id=peer(axis, k), device_id_type=MESH
        )

    own_copy = pltpu.make_async_copy(factor, own_rows, own_sem)
    own_copy.start()
    vectors[0] = jnp.zeros((k_all, nb), F32)
    vectors[1] = initial[...].T

    barrier = pltpu.get_barrier_semaphore()
    for axis in (X, Y):
        for k in (1, 2, 3):
            pl.semaphore_signal(barrier, inc=1, device_id=peer(axis, k), device_id_type=MESH)
    pl.semaphore_wait(barrier, 6)

    def rows_of(chain):
        return pl.ds(chain * kc, kc)

    def rs_copy(chain, axis, k):
        return remote(
            partial_out.at[chain, axis, k], partial_in.at[chain, axis, k],
            rs_send.at[chain, axis, k], rs_recv.at[chain, axis, k], axis, k,
        )

    def ag_copy(chain, axis, k, order):
        return remote(
            vectors.at[order + 1, rows_of(chain)], gathered.at[chain, axis, k],
            ag_send.at[chain, axis, k], ag_recv.at[chain, axis, k], axis, k,
        )

    def block_copy(ky, kx, axis):
        return remote(
            factor.at[:, pl.ds(column(ky, kx), nb)], arrived.at[ky, kx],
            block_send.at[ky, kx], block_recv.at[ky, kx], axis, kx if axis == X else ky,
        )

    half = nb // 2
    top_copy = remote(
        factor.at[pl.ds(0, half), pl.ds(column(2, 2), nb)], arrived.at[2, 2, pl.ds(0, half)],
        block_send.at[2, 2], block_recv.at[2, 2], X, 2,
    )
    side_copy = remote(
        factor.at[:, pl.ds(pl.multiple_of(column(2, 2) + half, half), half)], arrived_half,
        block_send.at[0, 0], block_recv.at[0, 0], Y, 2,
    )

    for chain in range(CHAINS):
        for k in (2, 1, 3):
            ag_copy(chain, 1 - FIRST[chain], k, 0).start()
    block_copies = []
    for over_x, over_y in zip(OVER_X, OVER_Y):
        block_copies += [(over_x, X), (over_y, Y)]
    for (ky, kx), axis in block_copies:
        block_copy(ky, kx, axis).start()
    top_copy.start()
    side_copy.start()

    def put(axis, k_out, k_in, rows, columns, value):
        high, low = split(value)
        w_high[axis, k_out, pl.ds(k_in * nb + rows[0], rows[1]), pl.ds(columns[0], columns[1])] = high
        w_low[axis, k_out, pl.ds(k_in * nb + rows[0], rows[1]), pl.ds(columns[0], columns[1])] = low

    whole = (0, nb)

    def place(ky, kx, value, axis):
        if axis == X:
            put(Y, ky, kx, whole, whole, value)
            put(X, kx, ky, whole, whole, value.T)
        else:
            put(X, kx, ky, whole, whole, value)
            put(Y, ky, kx, whole, whole, value.T)

    own_copy.wait()
    for k in range(SIDE):
        place(k, 0, own_rows[:, pl.ds(column(k, 0), nb)], X)
        if k:
            place(0, k, own_rows[:, pl.ds(column(0, k), nb)], Y)
    for (ky, kx), axis in block_copies:
        block_copy(ky, kx, axis).wait_recv()
        place(ky, kx, arrived[ky, kx], axis)
    top_copy.wait_recv()
    top = arrived[2, 2, pl.ds(0, half)]
    put(Y, 2, 2, (0, half), whole, top)
    put(X, 2, 2, whole, (0, half), top.T)
    side_copy.wait_recv()
    side = arrived_half[...]
    put(X, 2, 2, whole, (half, half), side)
    put(Y, 2, 2, (half, half), whole, side.T)

    low_end, high_end = bounds[0], bounds[1]
    centre = (low_end + high_end) / 2.0
    radius = (high_end - low_end) / 2.0

    def stack(chain, k, value):
        high, low = split(value)
        stacked[chain, pl.ds(0, kc), pl.ds(k * nb, nb)] = high
        stacked[chain, pl.ds(kc, kc), pl.ds(k * nb, nb)] = low

    def multiply(chain, axis, order):
        along = 1 - axis
        stack(chain, 0, vectors[order + 1, rows_of(chain)])
        for k in (1, 3, 2):
            ag_copy(chain, along, k, order).wait_recv()
            stack(chain, k, gathered[chain, along, k])
        for k in (2, 1, 3, 0):
            both = lax.dot_general(stacked[chain], w_high[axis, k], NN, preferred_element_type=F32)
            rest = lax.dot_general(stacked[chain, pl.ds(0, kc)], w_low[axis, k], NN, preferred_element_type=F32)
            part = both[:kc] + (both[kc:] + rest)
            if k:
                partial_out[chain, axis, k] = part
                rs_copy(chain, axis, k).start()
            else:
                partial_own[chain] = part
        for k in (1, 2, 3):
            ag_copy(chain, along, k, order).wait_send()

    def total(chain, axis):
        for k in (1, 3, 2):
            rs_copy(chain, axis, k).wait_recv()
        return (partial_own[chain] + partial_in[chain, axis, 1]) + (partial_in[chain, axis, 2] + partial_in[chain, axis, 3])

    def advance(chain, axis, order, twice):
        product = total(chain, axis)
        current = vectors[order + 1, rows_of(chain)]
        scaled = (product - centre * current) / radius
        vectors[order + 2, rows_of(chain)] = twice * scaled - vectors[order, rows_of(chain)]
        for k in (2, 1, 3):
            ag_copy(chain, axis, k, order + 1).start()
        for k in (1, 2, 3):
            rs_copy(chain, axis, k).wait_send()

    def pair(step, carry):
        for later in (0, 1):
            order = 2 * step + later
            twice = jnp.where(order == 0, 1.0, 2.0)
            for chain in range(CHAINS):
                multiply(chain, (FIRST[chain] + later) % 2, order)
            for chain in range(CHAINS):
                advance(chain, (FIRST[chain] + later) % 2, order, twice)
        return carry

    lax.fori_loop(0, DEGREE // 2, pair, 0)

    hk = k_all // 2

    def small_copy(which, stage, part, k):
        axis = (part + stage) % 2
        return remote(
            small_out.at[which, stage, pl.ds(part * hk, hk)], small_in.at[which, stage, k, pl.ds(part * hk, hk)],
            small_send.at[which, stage, part, k], small_recv.at[which, stage, part, k], axis, k,
        )

    def small_start(which, stage):
        for k in (2, 1, 3):
            for part in (0, 1):
                small_copy(which, stage, part, k).start()

    def small_sum(which, stage):
        for k in (1, 3, 2):
            for part in (0, 1):
                small_copy(which, stage, part, k).wait_recv()
        return (small_out[which, stage] + small_in[which, stage, 1]) + (small_in[which, stage, 2] + small_in[which, stage, 3])

    filtered = vectors[DEGREE + 1]
    small_out[0, 0] = exact_dot(filtered, filtered, NT)
    small_start(0, 0)
    for chain in range(CHAINS):
        multiply(chain, FIRST[chain], DEGREE)
    small_out[0, 1] = small_sum(0, 0)
    small_start(0, 1)
    for chain in range(CHAINS):
        vectors[0, rows_of(chain)] = total(chain, FIRST[chain])
    gram = small_sum(0, 1)

    row_at = lax.broadcasted_iota(jnp.int32, (k_all, k_all), 0)
    column_at = lax.broadcasted_iota(jnp.int32, (k_all, k_all), 1)
    diagonal = jnp.where(row_at == column_at, gram, 0.0)
    scale_rows = lax.rsqrt(jnp.sum(diagonal, axis=1, keepdims=True))
    scale_columns = lax.rsqrt(jnp.sum(diagonal, axis=0, keepdims=True))
    filtered = filtered * scale_rows
    image = vectors[0] * scale_rows
    small_out[1, 0] = exact_dot(filtered, image, NT)
    small_start(1, 0)

    work[:, pl.ds(0, k_all)] = gram * scale_rows * scale_columns
    work[:, pl.ds(k_all, k_all)] = jnp.where(row_at == column_at, 1.0, 0.0)
    panel_row = lax.broadcasted_iota(jnp.int32, (PANEL, 1), 0)

    def eliminate(panel):
        rows = pl.ds(panel * PANEL, PANEL)
        block = work[rows, :]
        for j in range(PANEL):
            at = panel * PANEL + j
            inverse = lax.rsqrt(block[j : j + 1, at : at + 1])
            pivot_row = block[j : j + 1, :] * inverse
            multiplier = jnp.where(panel_row > j, block[:, at : at + 1] * inverse, 0.0)
            block = jnp.where(panel_row == j, pivot_row, block - multiplier * pivot_row)
        work[rows, :] = block
        done = (panel + 1) * PANEL
        if done < k_all:
            below = pl.ds(done, k_all - done)
            work[below, :] = work[below, :] - exact_dot(block[:, done:k_all], block, TN)

    panels = k_all // PANEL
    for panel in range(panels // 2):
        eliminate(panel)
    small_out[1, 1] = small_sum(1, 0)
    small_start(1, 1)
    for panel in range(panels // 2, panels):
        eliminate(panel)
    inverse_low = work[:, pl.ds(k_all, k_all)]
    basis = exact_dot(inverse_low, filtered, NN)
    mapped = exact_dot(inverse_low, image, NN)
    basis_out[...] = basis.T
    inner = small_sum(1, 1)
    projected = exact_dot(exact_dot(inverse_low, inner, NN), inverse_low, NT)
    projected_out[...] = projected
    residual_out[...] = (mapped - exact_dot(projected, basis, TN)).T

    for (ky, kx), axis in block_copies:
        block_copy(ky, kx, axis).wait_send()
    top_copy.wait_send()
    side_copy.wait_send()
    for chain in range(CHAINS):
        for k in (1, 2, 3):
            rs_copy(chain, FIRST[chain], k).wait_send()
    for which in (0, 1):
        for stage in (0, 1):
            for part in (0, 1):
                for k in (1, 2, 3):
                    small_copy(which, stage, part, k).wait_send()


def local(factor, initial, bounds):
    nb, k_all = initial.shape
    kc = k_all // CHAINS
    vmem = pl.BlockSpec(memory_space=pltpu.VMEM)
    dma = pltpu.SemaphoreType.DMA
    return pl.pallas_call(
        kernel,
        out_shape=(
            jax.ShapeDtypeStruct((nb, k_all), F32),
            jax.ShapeDtypeStruct((k_all, k_all), F32),
            jax.ShapeDtypeStruct((nb, k_all), F32),
        ),
        in_specs=[pl.BlockSpec(memory_space=pl.ANY), vmem, pl.BlockSpec(memory_space=pltpu.SMEM)],
        out_specs=(vmem, vmem, vmem),
        scratch_shapes=[
            pltpu.VMEM((nb, SIDE * SIDE * nb), F32),
            pltpu.VMEM((SIDE, SIDE, nb, nb), F32),
            pltpu.VMEM((nb, nb // 2), F32),
            pltpu.VMEM((2, SIDE, SIDE * nb, nb), BF16),
            pltpu.VMEM((2, SIDE, SIDE * nb, nb), BF16),
            pltpu.VMEM((DEGREE + 2, k_all, nb), F32),
            pltpu.VMEM((CHAINS, 2 * kc, SIDE * nb), BF16),
            pltpu.VMEM((CHAINS, kc, nb), F32),
            pltpu.VMEM((CHAINS, 2, SIDE, kc, nb), F32),
            pltpu.VMEM((CHAINS, 2, SIDE, kc, nb), F32),
            pltpu.VMEM((CHAINS, 2, SIDE, kc, nb), F32),
            pltpu.VMEM((2, 2, k_all, k_all), F32),
            pltpu.VMEM((2, 2, SIDE, k_all, k_all), F32),
            pltpu.VMEM((k_all, 2 * k_all), F32),
            dma,
            dma((SIDE, SIDE)),
            dma((SIDE, SIDE)),
            dma((CHAINS, 2, SIDE)),
            dma((CHAINS, 2, SIDE)),
            dma((CHAINS, 2, SIDE)),
            dma((CHAINS, 2, SIDE)),
            dma((2, 2, 2, SIDE)),
            dma((2, 2, 2, SIDE)),
        ],
        compiler_params=pltpu.CompilerParams(collective_id=0, has_side_effects=True, vmem_limit_bytes=48 << 20),
    )(factor, initial, bounds)


def solution(mesh):
    in_specs = (P(("bulk", "blk"), None), P(("bulk", "blk"), None), P("bulk"))
    out_specs = (P(("bulk", "blk"), None), P("bulk", None), P(("bulk", "blk"), None))
    return jax.shard_map(local, mesh=mesh, in_specs=in_specs, out_specs=out_specs, check_vma=False)
```

```python
import functools

import jax
import jax.numpy as jnp
from jax import lax
from jax.experimental import pallas as pl
from jax.experimental.pallas import tpu as pltpu
from jax.sharding import PartitionSpec as P

DEGREE = 8
SIDE = 4
CHAINS = 4
PANEL = 32
GROUP = 16
DOWN = 2.0**-12
X, Y = 0, 1
FIRST = (X, Y, X, Y)
MESH = pl.DeviceIdType.MESH
F32, BF16 = jnp.float32, jnp.bfloat16
HIGHEST = lax.Precision.HIGHEST
NN = (((1,), (0,)), ((), ()))
NT = (((1,), (1,)), ((), ()))
TN = (((0,), (0,)), ((), ()))

OVER_X = ((1, 1), (3, 3), (2, 1), (2, 3))
OVER_Y = ((1, 3), (3, 1), (1, 2), (3, 2))
LOCAL = ((0, 0), (1, 0), (2, 0), (3, 0), (0, 1), (0, 2), (0, 3))


def exact_dot(left, right, dims):
    return lax.dot_general(left, right, dims, precision=HIGHEST, preferred_element_type=F32)


def xor(value, k):
    if k == 0:
        return value
    if k == 1:
        return value + 1 - 2 * (value % 2)
    if k == 2:
        return (value + 2) % 4
    return 3 - value


def split(value):
    high = value.astype(BF16)
    low = (value - high.astype(F32)).astype(BF16)
    return high, low


def kernel(
    factor, initial, bounds,
    basis_out, projected_out, residual_out,
    own_blocks, arrived, arrived_half, start, w_high, w_low, vectors, stacked, partial, sums, from_first, from_second,
    last_in, image_own, small_out, small_in, work, staged,
    own_sem, block_send, block_recv, x_send, x_recv, last_send, last_recv, small_send, small_recv,
):
    me = lax.axis_index("blk")
    my_y, my_x = me // SIDE, me % SIDE
    nb, k_all = start.shape[1], start.shape[0]
    kc = k_all // CHAINS
    hc = kc // 2
    half = nb // 2

    def peer(axis, k):
        if axis == X:
            return {"blk": my_y * SIDE + xor(my_x, k)}
        return {"blk": xor(my_y, k) * SIDE + my_x}

    def column(ky, kx):
        return pl.multiple_of((xor(my_y, ky) * SIDE + xor(my_x, kx)) * nb, nb)

    def remote(src, dst, send, recv, axis, k):
        return pltpu.make_async_remote_copy(
            src_ref=src, dst_ref=dst, send_sem=send, recv_sem=recv, device_id=peer(axis, k), device_id_type=MESH
        )

    def own_copy(at):
        ky, kx = LOCAL[at]
        return pltpu.make_async_copy(factor.at[:, pl.ds(column(ky, kx), nb)], own_blocks.at[at], own_sem.at[at])

    initial_copy = pltpu.make_async_copy(initial, staged, own_sem.at[len(LOCAL)])
    initial_copy.start()
    for at in range(len(LOCAL)):
        own_copy(at).start()

    barrier = pltpu.get_barrier_semaphore()
    for axis in (X, Y):
        for k in (1, 2, 3):
            pl.semaphore_signal(barrier, inc=1, device_id=peer(axis, k), device_id_type=MESH)

    low_end, high_end = bounds[0], bounds[1]
    centre = (low_end + high_end) / 2.0
    radius = (high_end - low_end) / 2.0
    scale = 2.0 / radius

    def put(axis, k_out, k_in, rows, columns, value):
        high, low = split(value)
        w_high[axis, k_out, pl.ds(k_in * nb + rows[0], rows[1]), pl.ds(columns[0], columns[1])] = high
        w_low[axis, k_out, pl.ds(k_in * nb + rows[0], rows[1]), pl.ds(columns[0], columns[1])] = low

    whole = (0, nb)

    def place(ky, kx, value, axis):
        value = value * scale
        if axis == X:
            put(Y, ky, kx, whole, whole, value)
            put(X, kx, ky, whole, whole, value.T)
        else:
            put(X, kx, ky, whole, whole, value)
            put(Y, ky, kx, whole, whole, value.T)

    initial_copy.wait()
    start[...] = staged[...].T
    for chain in range(CHAINS):
        vectors[chain, FIRST[chain]] = jnp.zeros((kc, SIDE * nb), F32)

    pl.semaphore_wait(barrier, 6)

    def rows_of(chain):
        return pl.ds(chain * kc, kc)

    def slot(k):
        return pl.ds(k * nb, nb)

    def first_copy(chain, k):
        axis = 1 - FIRST[chain]
        return remote(
            start.at[rows_of(chain)], vectors.at[chain, axis, :, slot(k)],
            last_send.at[0, chain, k], last_recv.at[0, chain, k], axis, k,
        )

    def last_copy(chain, k):
        axis = FIRST[chain]
        return remote(
            partial.at[chain, axis, :, slot(k)], last_in.at[chain, k],
            last_send.at[1, chain, k], last_recv.at[1, chain, k], axis, k,
        )

    def block_copy(ky, kx, axis):
        return remote(
            factor.at[:, pl.ds(column(ky, kx), nb)], arrived.at[ky, kx],
            block_send.at[ky, kx], block_recv.at[ky, kx], axis, kx if axis == X else ky,
        )

    top_copy = remote(
        factor.at[pl.ds(0, half), pl.ds(column(2, 2), nb)], arrived.at[2, 2, pl.ds(0, half)],
        block_send.at[2, 2], block_recv.at[2, 2], X, 2,
    )
    side_copy = remote(
        factor.at[:, pl.ds(pl.multiple_of(column(2, 2) + half, half), half)], arrived_half,
        block_send.at[0, 0], block_recv.at[0, 0], Y, 2,
    )

    for chain in range(CHAINS):
        for k in (2, 1, 3):
            first_copy(chain, k).start()
    block_copies = []
    for over_x, over_y in zip(OVER_X, OVER_Y):
        block_copies += [(over_x, X), (over_y, Y)]
    for (ky, kx), axis in block_copies:
        block_copy(ky, kx, axis).start()
    top_copy.start()
    side_copy.start()

    for at, (ky, kx) in enumerate(LOCAL):
        own_copy(at).wait()
        value = own_blocks[at]
        if at == 0:
            row_at = lax.broadcasted_iota(jnp.int32, (nb, nb), 0)
            column_at = lax.broadcasted_iota(jnp.int32, (nb, nb), 1)
            value = jnp.where(row_at == column_at, value - centre, value)
        place(ky, kx, value, X if kx == 0 else Y)

    def stack(chain, k, value):
        high, low = split(value)
        stacked[chain, pl.ds(0, kc), slot(k)] = high
        stacked[chain, pl.ds(kc, kc), slot(k)] = low

    for chain in range(CHAINS):
        axis = 1 - FIRST[chain]
        vectors[chain, axis, :, slot(0)] = start[rows_of(chain)]
        for k in (1, 3, 2):
            first_copy(chain, k).wait()
        for k in range(SIDE):
            stack(chain, k, vectors[chain, axis, :, slot(k)])
    for (ky, kx), axis in block_copies:
        block_copy(ky, kx, axis).wait_recv()
        place(ky, kx, arrived[ky, kx], axis)
    top_copy.wait_recv()
    top = arrived[2, 2, pl.ds(0, half)] * scale
    put(Y, 2, 2, (0, half), whole, top)
    put(X, 2, 2, whole, (0, half), top.T)
    side_copy.wait_recv()
    side = arrived_half[...] * scale
    put(X, 2, 2, whole, (half, half), side)
    put(Y, 2, 2, (half, half), whole, side.T)

    def parts():
        return ((0, 1, 3), (1, 3, 1))

    def exchange(chain, axis, order, stage, part):
        which, first, second = parts()[part]
        rows = pl.ds(which * hc, hc)
        source = (partial, sums)[stage].at[chain, axis, rows]
        target = (from_first, from_second)[stage].at[order % 4, chain, rows]
        return remote(
            source, target, x_send.at[order % 4, chain, stage, part], x_recv.at[order % 4, chain, stage, part],
            axis, (first, second)[stage],
        )

    def multiply(chain, axis, send):
        for k in (1, 2, 3, 0):
            both = lax.dot_general(stacked[chain], w_high[axis, k], NN, preferred_element_type=F32)
            rest = lax.dot_general(stacked[chain, pl.ds(0, kc)], w_low[axis, k], NN, preferred_element_type=F32)
            partial[chain, axis, :, slot(k)] = both[:kc] + (both[kc:] + rest)
            if send is None and k:
                last_copy(chain, k).start()
        if send is not None:
            for part in (0, 1):
                exchange(chain, axis, send, 0, part).start()

    def middle(chain, axis, order):
        for part, (which, first, _) in enumerate(parts()):
            rows = pl.ds(which * hc, hc)
            exchange(chain, axis, order, 0, part).wait_recv()
            for k in range(SIDE):
                sums[chain, axis, rows, slot(k)] = (
                    partial[chain, axis, rows, slot(k)] + from_first[order % 4, chain, rows, slot(k ^ first)]
                )
            exchange(chain, axis, order, 1, part).start()

    def advance(chain, axis, order, factor_of):
        for part, (which, _, second) in enumerate(parts()):
            rows = pl.ds(which * hc, hc)
            exchange(chain, axis, order, 1, part).wait_recv()
            for k in range(SIDE):
                product = sums[chain, axis, rows, slot(k)] + from_second[order % 4, chain, rows, slot(k ^ second)]
                value = factor_of * product - vectors[chain, axis, rows, slot(k)]
                vectors[chain, axis, rows, slot(k)] = value
                high, low = split(value)
                stacked[chain, rows, slot(k)] = high
                stacked[chain, pl.ds(kc + which * hc, hc), slot(k)] = low

    def settle(chain, axis, order):
        for stage in (0, 1):
            for part in (0, 1):
                exchange(chain, axis, order, stage, part).wait_send()

    def axis_of(chain, later):
        return (FIRST[chain] + later) % 2

    for chain in range(CHAINS):
        multiply(chain, FIRST[chain], 0)

    def pair(step, carry):
        order = 2 * step
        factor_of = jnp.where(step == 0, 0.5, 1.0)
        for chain in range(CHAINS):
            middle(chain, axis_of(chain, 0), order)
        for chain in range(CHAINS):
            advance(chain, axis_of(chain, 0), order, factor_of)
            multiply(chain, axis_of(chain, 1), order + 1)
            settle(chain, axis_of(chain, 0), order)
        for chain in range(CHAINS):
            middle(chain, axis_of(chain, 1), order + 1)

        if isinstance(step, int):
            return carry
        for chain in range(CHAINS):
            advance(chain, axis_of(chain, 1), order + 1, 1.0)
            multiply(chain, axis_of(chain, 0), order + 2)
            settle(chain, axis_of(chain, 1), order + 1)
        return carry

    lax.fori_loop(0, DEGREE // 2 - 1, pair, 0)
    pair(DEGREE // 2 - 1, 0)
    for chain in range(CHAINS):
        advance(chain, axis_of(chain, 1), DEGREE - 1, 1.0)
        start[rows_of(chain)] = vectors[chain, axis_of(chain, 1), :, slot(0)]

    hk = k_all // 2

    def small_copy(which, stage, part, k):
        axis = (part + stage) % 2
        return remote(
            small_out.at[which, stage, pl.ds(part * hk, hk)], small_in.at[which, stage, k, pl.ds(part * hk, hk)],
            small_send.at[which, stage, part, k], small_recv.at[which, stage, part, k], axis, k,
        )

    def small_start(which, stage):
        for k in (2, 1, 3):
            for part in (0, 1):
                small_copy(which, stage, part, k).start()

    def small_sum(which, stage):
        for k in (1, 3, 2):
            for part in (0, 1):
                small_copy(which, stage, part, k).wait_recv()
        return (small_out[which, stage] + small_in[which, stage, 1]) + (small_in[which, stage, 2] + small_in[which, stage, 3])

    filtered = start[...]
    small_out[0, 0] = exact_dot(filtered, filtered, NT)
    small_start(0, 0)
    for chain in range(CHAINS):
        multiply(chain, FIRST[chain], None)
        settle(chain, axis_of(chain, 1), DEGREE - 1)
    small_out[0, 1] = small_sum(0, 0)
    small_start(0, 1)
    for chain in range(CHAINS):
        for k in (1, 3, 2):
            last_copy(chain, k).wait_recv()
        product = (partial[chain, FIRST[chain], :, slot(0)] + last_in[chain, 1]) + (last_in[chain, 2] + last_in[chain, 3])
        image_own[rows_of(chain)] = product
    image = image_own[...] * (0.5 * radius) + centre * filtered
    small_out[1, 0] = exact_dot(filtered * DOWN, image * DOWN, NT)
    small_start(1, 0)
    gram = small_sum(0, 1)

    row_at = lax.broadcasted_iota(jnp.int32, (k_all, k_all), 0)
    column_at = lax.broadcasted_iota(jnp.int32, (k_all, k_all), 1)

    work[:, pl.ds(0, k_all)] = gram
    work[:, pl.ds(k_all, k_all)] = jnp.where(row_at == column_at, 1.0, 0.0)
    panel_row = lax.broadcasted_iota(jnp.int32, (PANEL, k_all), 0)

    def eliminate(panel):
        rows = pl.ds(panel * PANEL, PANEL)
        left, right = work[rows, pl.ds(0, k_all)], work[rows, pl.ds(k_all, k_all)]
        for group in range(0, PANEL, GROUP):
            at = panel * PANEL + group
            spread = [jnp.broadcast_to(left[:, at + t : at + t + 1], (PANEL, k_all)) for t in range(GROUP)]
            for t in range(GROUP):
                j = group + t
                inverse = lax.rsqrt(spread[t][j : j + 1, :])
                multiplier = jnp.where(panel_row > j, spread[t], 0.0) * inverse
                for later in range(t + 1, GROUP):
                    spread[later] = spread[later] - multiplier * (spread[later][j : j + 1, :] * inverse)
                left_row, right_row = left[j : j + 1, :] * inverse, right[j : j + 1, :] * inverse
                left = jnp.where(panel_row == j, left_row, left - multiplier * left_row)
                right = jnp.where(panel_row == j, right_row, right - multiplier * right_row)
        work[rows, pl.ds(0, k_all)] = left
        work[rows, pl.ds(k_all, k_all)] = right
        done = (panel + 1) * PANEL
        if done < k_all:
            below = pl.ds(done, k_all - done)
            work[below, :] = work[below, :] - exact_dot(left[:, done:k_all], work[rows, :], TN)

    panels = k_all // PANEL
    for panel in range(panels // 2):
        eliminate(panel)
    small_out[1, 1] = small_sum(1, 0)
    small_start(1, 1)
    for panel in range(panels // 2, panels):
        eliminate(panel)
    inverse_low = work[:, pl.ds(k_all, k_all)]
    basis = exact_dot(inverse_low, filtered, NN)
    mapped = exact_dot(inverse_low, image, NN)
    basis_out[...] = basis.T
    inner = small_sum(1, 1)
    projected = exact_dot(exact_dot(inverse_low / DOWN, inner, NN), inverse_low / DOWN, NT)
    projected_out[...] = projected
    residual_out[...] = (mapped - exact_dot(projected, basis, TN)).T

    for (ky, kx), axis in block_copies:
        block_copy(ky, kx, axis).wait_send()
    top_copy.wait_send()
    side_copy.wait_send()
    for chain in range(CHAINS):
        for k in (1, 2, 3):
            last_copy(chain, k).wait_send()
    for which in (0, 1):
        for stage in (0, 1):
            for part in (0, 1):
                for k in (1, 2, 3):
                    small_copy(which, stage, part, k).wait_send()


def local(factor, initial, bounds):
    nb, k_all = initial.shape
    kc = k_all // CHAINS
    vmem = pl.BlockSpec(memory_space=pltpu.VMEM)
    hbm = pl.BlockSpec(memory_space=pltpu.HBM)
    dma = pltpu.SemaphoreType.DMA
    long = SIDE * nb
    return pl.pallas_call(
        kernel,
        out_shape=(
            jax.ShapeDtypeStruct((nb, k_all), F32),
            jax.ShapeDtypeStruct((k_all, k_all), F32),
            jax.ShapeDtypeStruct((nb, k_all), F32),
        ),
        in_specs=[hbm, hbm, pl.BlockSpec(memory_space=pltpu.SMEM)],
        out_specs=(vmem, vmem, vmem),
        scratch_shapes=[
            pltpu.VMEM((len(LOCAL), nb, nb), F32),
            pltpu.VMEM((SIDE, SIDE, nb, nb), F32),
            pltpu.VMEM((nb, nb // 2), F32),
            pltpu.VMEM((k_all, nb), F32),
            pltpu.VMEM((2, SIDE, long, nb), BF16),
            pltpu.VMEM((2, SIDE, long, nb), BF16),
            pltpu.VMEM((CHAINS, 2, kc, long), F32),
            pltpu.VMEM((CHAINS, 2 * kc, long), BF16),
            pltpu.VMEM((CHAINS, 2, kc, long), F32),
            pltpu.VMEM((CHAINS, 2, kc, long), F32),
            pltpu.VMEM((4, CHAINS, kc, long), F32),
            pltpu.VMEM((4, CHAINS, kc, long), F32),
            pltpu.VMEM((CHAINS, SIDE, kc, nb), F32),
            pltpu.VMEM((k_all, nb), F32),
            pltpu.VMEM((2, 2, k_all, k_all), F32),
            pltpu.VMEM((2, 2, SIDE, k_all, k_all), F32),
            pltpu.VMEM((k_all, 2 * k_all), F32),
            pltpu.VMEM((nb, k_all), F32),
            dma((len(LOCAL) + 1,)),
            dma((SIDE, SIDE)),
            dma((SIDE, SIDE)),
            dma((4, CHAINS, 2, 2)),
            dma((4, CHAINS, 2, 2)),
            dma((2, CHAINS, SIDE)),
            dma((2, CHAINS, SIDE)),
            dma((2, 2, 2, SIDE)),
            dma((2, 2, 2, SIDE)),
        ],
        compiler_params=pltpu.CompilerParams(collective_id=0, has_side_effects=True, vmem_limit_bytes=61 << 20),
    )(factor, initial, bounds)


def solution(mesh):
    in_specs = (P(("bulk", "blk"), None), P(("bulk", "blk"), None), P("bulk"))
    out_specs = (P(("bulk", "blk"), None), P("bulk", None), P(("bulk", "blk"), None))
    return jax.shard_map(local, mesh=mesh, in_specs=in_specs, out_specs=out_specs, check_vma=False)
```

```python
import functools

import jax
import jax.numpy as jnp
from jax import lax
from jax.experimental import pallas as pl
from jax.experimental.pallas import tpu as pltpu
from jax.sharding import PartitionSpec as P

DEGREE = 8
SIDE = 4
CHAINS = 4
PANEL = 32
GROUP = 16
DOWN = 2.0**-12
X, Y = 0, 1
FIRST = (X, Y, X, Y)
MESH = pl.DeviceIdType.MESH
F32, BF16 = jnp.float32, jnp.bfloat16
HIGHEST = lax.Precision.HIGHEST
NN = (((1,), (0,)), ((), ()))
NT = (((1,), (1,)), ((), ()))
TN = (((0,), (0,)), ((), ()))

OVER_X = ((1, 1), (3, 3), (2, 1), (2, 3))
OVER_Y = ((1, 3), (3, 1), (1, 2), (3, 2))
LOCAL = ((0, 0), (1, 0), (2, 0), (3, 0), (0, 1), (0, 2), (0, 3))


def exact_dot(left, right, dims):
    return lax.dot_general(left, right, dims, precision=HIGHEST, preferred_element_type=F32)


def xor(value, k):
    if k == 0:
        return value
    if k == 1:
        return value + 1 - 2 * (value % 2)
    if k == 2:
        return (value + 2) % 4
    return 3 - value


def split(value):
    high = value.astype(BF16)
    low = (value - high.astype(F32)).astype(BF16)
    return high, low


def kernel(
    factor, initial, bounds,
    basis_out, projected_out, residual_out,
    own_blocks, arrived, arrived_half, start, w_high, w_low, vectors, stacked, partial, sums, from_first, from_second,
    last_in, image_own, small_out, small_in, work, staged,
    own_sem, block_send, block_recv, x_send, x_recv, last_send, last_recv, small_send, small_recv,
):
    me = lax.axis_index("blk")
    my_y, my_x = me // SIDE, me % SIDE
    nb, k_all = start.shape[1], start.shape[0]
    kc = k_all // CHAINS
    hc = kc // 2
    half = nb // 2

    def peer(axis, k):
        if axis == X:
            return {"blk": my_y * SIDE + xor(my_x, k)}
        return {"blk": xor(my_y, k) * SIDE + my_x}

    def column(ky, kx):
        return pl.multiple_of((xor(my_y, ky) * SIDE + xor(my_x, kx)) * nb, nb)

    def remote(src, dst, send, recv, axis, k):
        return pltpu.make_async_remote_copy(
            src_ref=src, dst_ref=dst, send_sem=send, recv_sem=recv, device_id=peer(axis, k), device_id_type=MESH
        )

    def own_copy(at):
        ky, kx = LOCAL[at]
        return pltpu.make_async_copy(factor.at[:, pl.ds(column(ky, kx), nb)], own_blocks.at[at], own_sem.at[at])

    initial_copy = pltpu.make_async_copy(initial, staged, own_sem.at[len(LOCAL)])
    initial_copy.start()
    for at in range(len(LOCAL)):
        own_copy(at).start()

    barrier = pltpu.get_barrier_semaphore()
    for axis in (X, Y):
        for k in (1, 2, 3):
            pl.semaphore_signal(barrier, inc=1, device_id=peer(axis, k), device_id_type=MESH)

    low_end, high_end = bounds[0], bounds[1]
    centre = (low_end + high_end) / 2.0
    radius = (high_end - low_end) / 2.0
    scale = 2.0 / radius

    def put(axis, k_out, k_in, rows, columns, value):
        high, low = split(value)
        w_high[axis, k_out, pl.ds(k_in * nb + rows[0], rows[1]), pl.ds(columns[0], columns[1])] = high
        w_low[axis, k_out, pl.ds(k_in * nb + rows[0], rows[1]), pl.ds(columns[0], columns[1])] = low

    whole = (0, nb)

    def place(ky, kx, value, axis):
        value = value * scale
        if axis == X:
            put(Y, ky, kx, whole, whole, value)
            put(X, kx, ky, whole, whole, value.T)
        else:
            put(X, kx, ky, whole, whole, value)
            put(Y, ky, kx, whole, whole, value.T)

    initial_copy.wait()
    start[...] = staged[...].T
    for chain in range(CHAINS):
        vectors[chain, FIRST[chain]] = jnp.zeros((kc, SIDE * nb), F32)

    pl.semaphore_wait(barrier, 6)

    def rows_of(chain):
        return pl.ds(chain * kc, kc)

    def slot(k):
        return pl.ds(k * nb, nb)

    def first_copy(chain, k):
        axis = 1 - FIRST[chain]
        return remote(
            start.at[rows_of(chain)], vectors.at[chain, axis, :, slot(k)],
            last_send.at[0, chain, k], last_recv.at[0, chain, k], axis, k,
        )

    def last_copy(chain, k):
        axis = FIRST[chain]
        return remote(
            partial.at[chain, axis, :, slot(k)], last_in.at[chain, k],
            last_send.at[1, chain, k], last_recv.at[1, chain, k], axis, k,
        )

    def block_copy(ky, kx, axis):
        return remote(
            factor.at[:, pl.ds(column(ky, kx), nb)], arrived.at[ky, kx],
            block_send.at[ky, kx], block_recv.at[ky, kx], axis, kx if axis == X else ky,
        )

    top_copy = remote(
        factor.at[pl.ds(0, half), pl.ds(column(2, 2), nb)], arrived.at[2, 2, pl.ds(0, half)],
        block_send.at[2, 2], block_recv.at[2, 2], X, 2,
    )
    side_copy = remote(
        factor.at[:, pl.ds(pl.multiple_of(column(2, 2) + half, half), half)], arrived_half,
        block_send.at[0, 0], block_recv.at[0, 0], Y, 2,
    )

    for chain in range(CHAINS):
        for k in (2, 1, 3):
            first_copy(chain, k).start()
    block_copies = []
    for over_x, over_y in zip(OVER_X, OVER_Y):
        block_copies += [(over_x, X), (over_y, Y)]
    for (ky, kx), axis in block_copies:
        block_copy(ky, kx, axis).start()
    top_copy.start()
    side_copy.start()

    for at, (ky, kx) in enumerate(LOCAL):
        own_copy(at).wait()
        value = own_blocks[at]
        if at == 0:
            row_at = lax.broadcasted_iota(jnp.int32, (nb, nb), 0)
            column_at = lax.broadcasted_iota(jnp.int32, (nb, nb), 1)
            value = jnp.where(row_at == column_at, value - centre, value)
        place(ky, kx, value, X if kx == 0 else Y)

    def stack(chain, k, value):
        high, low = split(value)
        stacked[chain, pl.ds(0, kc), slot(k)] = high
        stacked[chain, pl.ds(kc, kc), slot(k)] = low

    for chain in range(CHAINS):
        axis = 1 - FIRST[chain]
        vectors[chain, axis, :, slot(0)] = start[rows_of(chain)]
        for k in (1, 3, 2):
            first_copy(chain, k).wait()
        for k in range(SIDE):
            stack(chain, k, vectors[chain, axis, :, slot(k)])
    def parts():
        return ((0, 1, 3), (1, 3, 1))

    def exchange(chain, axis, order, stage, part):
        which, first, second = parts()[part]
        rows = pl.ds(which * hc, hc)
        source = (partial, sums)[stage].at[chain, axis, rows]
        target = (from_first, from_second)[stage].at[order % 4, chain, rows]
        return remote(
            source, target, x_send.at[order % 4, chain, stage, part], x_recv.at[order % 4, chain, stage, part],
            axis, (first, second)[stage],
        )

    def dots(chain, axis, slots):
        for k in slots:
            both = lax.dot_general(stacked[chain], w_high[axis, k], NN, preferred_element_type=F32)
            rest = lax.dot_general(stacked[chain, pl.ds(0, kc)], w_low[axis, k], NN, preferred_element_type=F32)
            partial[chain, axis, :, slot(k)] = both[:kc] + (both[kc:] + rest)

    def multiply(chain, axis, send):
        if send is None:
            for k in (2, 1, 3, 0):
                dots(chain, axis, (k,))
                if k:
                    last_copy(chain, k).start()
        else:
            dots(chain, axis, (0, 1, 2, 3))
            for part in (0, 1):
                exchange(chain, axis, send, 0, part).start()

    def middle(chain, axis, order):
        for part, (which, first, _) in enumerate(parts()):
            rows = pl.ds(which * hc, hc)
            exchange(chain, axis, order, 0, part).wait_recv()
            for k in range(SIDE):
                sums[chain, axis, rows, slot(k)] = (
                    partial[chain, axis, rows, slot(k)] + from_first[order % 4, chain, rows, slot(k ^ first)]
                )
            exchange(chain, axis, order, 1, part).start()

    def advance(chain, axis, order, factor_of):
        for part, (which, _, second) in enumerate(parts()):
            rows = pl.ds(which * hc, hc)
            exchange(chain, axis, order, 1, part).wait_recv()
            for k in range(SIDE):
                product = sums[chain, axis, rows, slot(k)] + from_second[order % 4, chain, rows, slot(k ^ second)]
                value = factor_of * product - vectors[chain, axis, rows, slot(k)]
                vectors[chain, axis, rows, slot(k)] = value
                high, low = split(value)
                stacked[chain, rows, slot(k)] = high
                stacked[chain, pl.ds(kc + which * hc, hc), slot(k)] = low

    def settle(chain, axis, order):
        for stage in (0, 1):
            for part in (0, 1):
                exchange(chain, axis, order, stage, part).wait_send()

    def axis_of(chain, later):
        return (FIRST[chain] + later) % 2

    for (ky, kx), axis in block_copies:
        block_copy(ky, kx, axis).wait_recv()
        place(ky, kx, arrived[ky, kx], axis)
    for chain in range(CHAINS):
        dots(chain, FIRST[chain], (0, 1, 3))
    top_copy.wait_recv()
    top = arrived[2, 2, pl.ds(0, half)] * scale
    put(Y, 2, 2, (0, half), whole, top)
    put(X, 2, 2, whole, (0, half), top.T)
    side_copy.wait_recv()
    side = arrived_half[...] * scale
    put(X, 2, 2, whole, (half, half), side)
    put(Y, 2, 2, (half, half), whole, side.T)

    for chain in range(CHAINS):
        dots(chain, FIRST[chain], (2,))
        for part in (0, 1):
            exchange(chain, FIRST[chain], 0, 0, part).start()

    def pair(step, carry):
        order = 2 * step
        factor_of = jnp.where(step == 0, 0.5, 1.0)
        for chain in range(CHAINS):
            middle(chain, axis_of(chain, 0), order)
        for chain in range(CHAINS):
            advance(chain, axis_of(chain, 0), order, factor_of)
            multiply(chain, axis_of(chain, 1), order + 1)
            settle(chain, axis_of(chain, 0), order)
        for chain in range(CHAINS):
            middle(chain, axis_of(chain, 1), order + 1)

        if isinstance(step, int):
            return carry
        for chain in range(CHAINS):
            advance(chain, axis_of(chain, 1), order + 1, 1.0)
            multiply(chain, axis_of(chain, 0), order + 2)
            settle(chain, axis_of(chain, 1), order + 1)
        return carry

    lax.fori_loop(0, DEGREE // 2 - 1, pair, 0)
    pair(DEGREE // 2 - 1, 0)
    for chain in range(CHAINS):
        advance(chain, axis_of(chain, 1), DEGREE - 1, 1.0)
        start[rows_of(chain)] = vectors[chain, axis_of(chain, 1), :, slot(0)]

    hk = k_all // 2

    def small_copy(which, stage, part, k):
        axis = (part + stage) % 2
        return remote(
            small_out.at[which, stage, pl.ds(part * hk, hk)], small_in.at[which, stage, k, pl.ds(part * hk, hk)],
            small_send.at[which, stage, part, k], small_recv.at[which, stage, part, k], axis, k,
        )

    def small_start(which, stage):
        for k in (2, 1, 3):
            for part in (0, 1):
                small_copy(which, stage, part, k).start()

    def small_sum(which, stage):
        for k in (1, 3, 2):
            for part in (0, 1):
                small_copy(which, stage, part, k).wait_recv()
        return (small_out[which, stage] + small_in[which, stage, 1]) + (small_in[which, stage, 2] + small_in[which, stage, 3])

    filtered = start[...]
    small_out[0, 0] = exact_dot(filtered, filtered, NT)
    small_start(0, 0)
    for chain in range(CHAINS):
        multiply(chain, FIRST[chain], None)
        settle(chain, axis_of(chain, 1), DEGREE - 1)
    small_out[0, 1] = small_sum(0, 0)
    small_start(0, 1)
    for chain in range(CHAINS):
        for k in (1, 3, 2):
            last_copy(chain, k).wait_recv()
        product = (partial[chain, FIRST[chain], :, slot(0)] + last_in[chain, 1]) + (last_in[chain, 2] + last_in[chain, 3])
        image_own[rows_of(chain)] = product
    image = image_own[...] * (0.5 * radius) + centre * filtered
    small_out[1, 0] = exact_dot(filtered * DOWN, image * DOWN, NT)
    small_start(1, 0)
    gram = small_sum(0, 1)

    row_at = lax.broadcasted_iota(jnp.int32, (k_all, k_all), 0)
    column_at = lax.broadcasted_iota(jnp.int32, (k_all, k_all), 1)

    work[:, pl.ds(0, k_all)] = gram
    work[:, pl.ds(k_all, k_all)] = jnp.where(row_at == column_at, 1.0, 0.0)
    panel_row = lax.broadcasted_iota(jnp.int32, (PANEL, k_all), 0)

    def eliminate(panel):
        rows = pl.ds(panel * PANEL, PANEL)
        left, right = work[rows, pl.ds(0, k_all)], work[rows, pl.ds(k_all, k_all)]
        for group in range(0, PANEL, GROUP):
            at = panel * PANEL + group
            spread = [jnp.broadcast_to(left[:, at + t : at + t + 1], (PANEL, k_all)) for t in range(GROUP)]
            for t in range(GROUP):
                j = group + t
                inverse = lax.rsqrt(spread[t][j : j + 1, :])
                multiplier = jnp.where(panel_row > j, spread[t], 0.0) * inverse
                for later in range(t + 1, GROUP):
                    spread[later] = spread[later] - multiplier * (spread[later][j : j + 1, :] * inverse)
                left_row, right_row = left[j : j + 1, :] * inverse, right[j : j + 1, :] * inverse
                left = jnp.where(panel_row == j, left_row, left - multiplier * left_row)
                right = jnp.where(panel_row == j, right_row, right - multiplier * right_row)
        work[rows, pl.ds(0, k_all)] = left
        work[rows, pl.ds(k_all, k_all)] = right
        done = (panel + 1) * PANEL
        if done < k_all:
            below = pl.ds(done, k_all - done)
            work[below, :] = work[below, :] - exact_dot(left[:, done:k_all], work[rows, :], TN)

    panels = k_all // PANEL
    for panel in range(panels // 2):
        eliminate(panel)
    small_out[1, 1] = small_sum(1, 0)
    small_start(1, 1)
    for panel in range(panels // 2, panels):
        eliminate(panel)
    inverse_low = work[:, pl.ds(k_all, k_all)]
    basis = exact_dot(inverse_low, filtered, NN)
    mapped = exact_dot(inverse_low, image, NN)
    basis_out[...] = basis.T
    inner = small_sum(1, 1)
    projected = exact_dot(exact_dot(inverse_low / DOWN, inner, NN), inverse_low / DOWN, NT)
    projected_out[...] = projected
    residual_out[...] = (mapped - exact_dot(projected, basis, TN)).T

    for (ky, kx), axis in block_copies:
        block_copy(ky, kx, axis).wait_send()
    top_copy.wait_send()
    side_copy.wait_send()
    for chain in range(CHAINS):
        for k in (1, 2, 3):
            last_copy(chain, k).wait_send()
    for which in (0, 1):
        for stage in (0, 1):
            for part in (0, 1):
                for k in (1, 2, 3):
                    small_copy(which, stage, part, k).wait_send()


def local(factor, initial, bounds):
    nb, k_all = initial.shape
    kc = k_all // CHAINS
    vmem = pl.BlockSpec(memory_space=pltpu.VMEM)
    hbm = pl.BlockSpec(memory_space=pltpu.HBM)
    dma = pltpu.SemaphoreType.DMA
    long = SIDE * nb
    return pl.pallas_call(
        kernel,
        out_shape=(
            jax.ShapeDtypeStruct((nb, k_all), F32),
            jax.ShapeDtypeStruct((k_all, k_all), F32),
            jax.ShapeDtypeStruct((nb, k_all), F32),
        ),
        in_specs=[hbm, hbm, pl.BlockSpec(memory_space=pltpu.SMEM)],
        out_specs=(vmem, vmem, vmem),
        scratch_shapes=[
            pltpu.VMEM((len(LOCAL), nb, nb), F32),
            pltpu.VMEM((SIDE, SIDE, nb, nb), F32),
            pltpu.VMEM((nb, nb // 2), F32),
            pltpu.VMEM((k_all, nb), F32),
            pltpu.VMEM((2, SIDE, long, nb), BF16),
            pltpu.VMEM((2, SIDE, long, nb), BF16),
            pltpu.VMEM((CHAINS, 2, kc, long), F32),
            pltpu.VMEM((CHAINS, 2 * kc, long), BF16),
            pltpu.VMEM((CHAINS, 2, kc, long), F32),
            pltpu.VMEM((CHAINS, 2, kc, long), F32),
            pltpu.VMEM((4, CHAINS, kc, long), F32),
            pltpu.VMEM((4, CHAINS, kc, long), F32),
            pltpu.VMEM((CHAINS, SIDE, kc, nb), F32),
            pltpu.VMEM((k_all, nb), F32),
            pltpu.VMEM((2, 2, k_all, k_all), F32),
            pltpu.VMEM((2, 2, SIDE, k_all, k_all), F32),
            pltpu.VMEM((k_all, 2 * k_all), F32),
            pltpu.VMEM((nb, k_all), F32),
            dma((len(LOCAL) + 1,)),
            dma((SIDE, SIDE)),
            dma((SIDE, SIDE)),
            dma((4, CHAINS, 2, 2)),
            dma((4, CHAINS, 2, 2)),
            dma((2, CHAINS, SIDE)),
            dma((2, CHAINS, SIDE)),
            dma((2, 2, 2, SIDE)),
            dma((2, 2, 2, SIDE)),
        ],
        compiler_params=pltpu.CompilerParams(collective_id=0, has_side_effects=True, vmem_limit_bytes=52 << 20),
    )(factor, initial, bounds)


def solution(mesh):
    in_specs = (P(("bulk", "blk"), None), P(("bulk", "blk"), None), P("bulk"))
    out_specs = (P(("bulk", "blk"), None), P("bulk", None), P(("bulk", "blk"), None))
    return jax.shard_map(local, mesh=mesh, in_specs=in_specs, out_specs=out_specs, check_vma=False)
```

```python
import functools

import jax
import jax.numpy as jnp
from jax import lax
from jax.experimental import pallas as pl
from jax.experimental.pallas import tpu as pltpu
from jax.sharding import PartitionSpec as P

DEGREE = 8
SIDE = 4
CHAINS = 4
PANEL = 32
GROUP = 16
DOWN = 2.0**-12
X, Y = 0, 1
FIRST = (X, Y, X, Y)
MESH = pl.DeviceIdType.MESH
F32, BF16 = jnp.float32, jnp.bfloat16
HIGHEST = lax.Precision.HIGHEST
NN = (((1,), (0,)), ((), ()))
NT = (((1,), (1,)), ((), ()))
TN = (((0,), (0,)), ((), ()))

OVER_X = ((1, 1), (3, 3), (2, 1), (2, 3))
OVER_Y = ((1, 3), (3, 1), (1, 2), (3, 2))
LOCAL = ((0, 0), (1, 0), (2, 0), (3, 0), (0, 1), (0, 2), (0, 3))


def exact_dot(left, right, dims):
    return lax.dot_general(left, right, dims, precision=HIGHEST, preferred_element_type=F32)


def xor(value, k):
    if k == 0:
        return value
    if k == 1:
        return value + 1 - 2 * (value % 2)
    if k == 2:
        return (value + 2) % 4
    return 3 - value


def split(value):
    high = value.astype(BF16)
    low = (value - high.astype(F32)).astype(BF16)
    return high, low


def kernel(
    factor, initial, bounds,
    basis_out, projected_out, residual_out,
    own_blocks, arrived, arrived_half, start, w_high, w_low, vectors, stacked, partial, sums, from_first, from_second,
    last_in, image_own, small_out, small_in, work, staged,
    own_sem, block_send, block_recv, x_send, x_recv, last_send, last_recv, small_send, small_recv,
):
    me = lax.axis_index("blk")
    my_y, my_x = me // SIDE, me % SIDE
    nb, k_all = start.shape[1], start.shape[0]
    kc = k_all // CHAINS
    hc = kc // 2
    half = nb // 2

    def peer(axis, k):
        if axis == X:
            return {"blk": my_y * SIDE + xor(my_x, k)}
        return {"blk": xor(my_y, k) * SIDE + my_x}

    def column(ky, kx):
        return pl.multiple_of((xor(my_y, ky) * SIDE + xor(my_x, kx)) * nb, nb)

    def remote(src, dst, send, recv, axis, k):
        return pltpu.make_async_remote_copy(
            src_ref=src, dst_ref=dst, send_sem=send, recv_sem=recv, device_id=peer(axis, k), device_id_type=MESH
        )

    def own_copy(at):
        ky, kx = LOCAL[at]
        return pltpu.make_async_copy(factor.at[:, pl.ds(column(ky, kx), nb)], own_blocks.at[at], own_sem.at[at])

    initial_copy = pltpu.make_async_copy(initial, staged, own_sem.at[len(LOCAL)])
    initial_copy.start()
    for at in range(len(LOCAL)):
        own_copy(at).start()

    barrier = pltpu.get_barrier_semaphore()
    for axis in (X, Y):
        for k in (1, 2, 3):
            pl.semaphore_signal(barrier, inc=1, device_id=peer(axis, k), device_id_type=MESH)

    low_end, high_end = bounds[0], bounds[1]
    centre = (low_end + high_end) / 2.0
    radius = (high_end - low_end) / 2.0
    scale = 2.0 / radius

    def put(axis, k_out, k_in, rows, columns, value):
        high, low = split(value)
        w_high[axis, k_out, pl.ds(k_in * nb + rows[0], rows[1]), pl.ds(columns[0], columns[1])] = high
        w_low[axis, k_out, pl.ds(k_in * nb + rows[0], rows[1]), pl.ds(columns[0], columns[1])] = low

    whole = (0, nb)

    def place(ky, kx, value, axis):
        value = value * scale
        if axis == X:
            put(Y, ky, kx, whole, whole, value)
            put(X, kx, ky, whole, whole, value.T)
        else:
            put(X, kx, ky, whole, whole, value)
            put(Y, ky, kx, whole, whole, value.T)

    initial_copy.wait()
    start[...] = staged[...].T
    for chain in range(CHAINS):
        vectors[chain, FIRST[chain]] = jnp.zeros((kc, SIDE * nb), F32)

    pl.semaphore_wait(barrier, 6)

    def rows_of(chain):
        return pl.ds(chain * kc, kc)

    def slot(k):
        return pl.ds(k * nb, nb)

    def first_copy(chain, k):
        axis = 1 - FIRST[chain]
        return remote(
            start.at[rows_of(chain)], vectors.at[chain, axis, :, slot(k)],
            last_send.at[0, chain, k], last_recv.at[0, chain, k], axis, k,
        )

    def last_copy(chain, k):
        axis = FIRST[chain]
        return remote(
            partial.at[chain, axis, :, slot(k)], last_in.at[chain, k],
            last_send.at[1, chain, k], last_recv.at[1, chain, k], axis, k,
        )

    def block_copy(ky, kx, axis):
        return remote(
            factor.at[:, pl.ds(column(ky, kx), nb)], arrived.at[ky, kx],
            block_send.at[ky, kx], block_recv.at[ky, kx], axis, kx if axis == X else ky,
        )

    top_copy = remote(
        factor.at[pl.ds(0, half), pl.ds(column(2, 2), nb)], arrived.at[2, 2, pl.ds(0, half)],
        block_send.at[2, 2], block_recv.at[2, 2], X, 2,
    )
    side_copy = remote(
        factor.at[:, pl.ds(pl.multiple_of(column(2, 2) + half, half), half)], arrived_half,
        block_send.at[0, 0], block_recv.at[0, 0], Y, 2,
    )

    for chain in range(CHAINS):
        for k in (2, 1, 3):
            first_copy(chain, k).start()
    block_copies = []
    for over_x, over_y in zip(OVER_X, OVER_Y):
        block_copies += [(over_x, X), (over_y, Y)]
    for (ky, kx), axis in block_copies:
        block_copy(ky, kx, axis).start()
    top_copy.start()
    side_copy.start()

    for at, (ky, kx) in enumerate(LOCAL):
        own_copy(at).wait()
        value = own_blocks[at]
        if at == 0:
            row_at = lax.broadcasted_iota(jnp.int32, (nb, nb), 0)
            column_at = lax.broadcasted_iota(jnp.int32, (nb, nb), 1)
            value = jnp.where(row_at == column_at, value - centre, value)
        place(ky, kx, value, X if kx == 0 else Y)

    def stack(chain, k, value):
        high, low = split(value)
        stacked[chain, pl.ds(0, kc), slot(k)] = high
        stacked[chain, pl.ds(kc, kc), slot(k)] = low

    for chain in range(CHAINS):
        axis = 1 - FIRST[chain]
        vectors[chain, axis, :, slot(0)] = start[rows_of(chain)]
        for k in (1, 3, 2):
            first_copy(chain, k).wait()
        for k in range(SIDE):
            stack(chain, k, vectors[chain, axis, :, slot(k)])
    def parts():
        return ((0, 1, 3), (1, 3, 1))

    def exchange(chain, axis, order, stage, part):
        which, first, second = parts()[part]
        rows = pl.ds(which * hc, hc)
        lanes = pl.ds((stage // 2) * 2 * nb, 2 * nb)
        source = (partial, sums)[stage % 2].at[chain, axis, rows, lanes]
        target = (from_first, from_second)[stage % 2].at[order % 4, chain, rows, lanes]
        return remote(
            source, target, x_send.at[order % 4, chain, stage, part], x_recv.at[order % 4, chain, stage, part],
            axis, (first, second)[stage % 2],
        )

    def dots(chain, axis, slots):
        for k in slots:
            both = lax.dot_general(stacked[chain], w_high[axis, k], NN, preferred_element_type=F32)
            rest = lax.dot_general(stacked[chain, pl.ds(0, kc)], w_low[axis, k], NN, preferred_element_type=F32)
            partial[chain, axis, :, slot(k)] = both[:kc] + (both[kc:] + rest)

    def multiply(chain, axis, send):
        if send is None:
            for k in (2, 1, 3, 0):
                dots(chain, axis, (k,))
                if k:
                    last_copy(chain, k).start()
        else:
            for piece in (0, 2):
                dots(chain, axis, (piece, piece + 1))
                for part in (0, 1):
                    exchange(chain, axis, send, piece, part).start()

    def middle(chain, axis, order):
        for piece in (0, 1):
            for part, (which, first, _) in enumerate(parts()):
                rows = pl.ds(which * hc, hc)
                exchange(chain, axis, order, 2 * piece, part).wait_recv()
                mine = piece if first == 1 else 1 - piece
                for k in (2 * mine, 2 * mine + 1):
                    sums[chain, axis, rows, slot(k)] = (
                        partial[chain, axis, rows, slot(k)] + from_first[order % 4, chain, rows, slot(k ^ first)]
                    )
                exchange(chain, axis, order, 2 * mine + 1, part).start()

    def advance(chain, axis, order, factor_of):
        for part, (which, _, second) in enumerate(parts()):
            rows = pl.ds(which * hc, hc)
            exchange(chain, axis, order, 1, part).wait_recv()
            exchange(chain, axis, order, 3, part).wait_recv()
            for k in range(SIDE):
                product = sums[chain, axis, rows, slot(k)] + from_second[order % 4, chain, rows, slot(k ^ second)]
                value = factor_of * product - vectors[chain, axis, rows, slot(k)]
                vectors[chain, axis, rows, slot(k)] = value
                high, low = split(value)
                stacked[chain, rows, slot(k)] = high
                stacked[chain, pl.ds(kc + which * hc, hc), slot(k)] = low

    def settle(chain, axis, order):
        for stage in range(4):
            for part in (0, 1):
                exchange(chain, axis, order, stage, part).wait_send()

    def axis_of(chain, later):
        return (FIRST[chain] + later) % 2

    for (ky, kx), axis in block_copies:
        block_copy(ky, kx, axis).wait_recv()
        place(ky, kx, arrived[ky, kx], axis)
    for chain in range(CHAINS):
        dots(chain, FIRST[chain], (0, 1, 3))
    top_copy.wait_recv()
    top = arrived[2, 2, pl.ds(0, half)] * scale
    put(Y, 2, 2, (0, half), whole, top)
    put(X, 2, 2, whole, (0, half), top.T)
    side_copy.wait_recv()
    side = arrived_half[...] * scale
    put(X, 2, 2, whole, (half, half), side)
    put(Y, 2, 2, (half, half), whole, side.T)

    for chain in range(CHAINS):
        dots(chain, FIRST[chain], (2,))
        for part in (0, 1):
            exchange(chain, FIRST[chain], 0, 0, part).start()
            exchange(chain, FIRST[chain], 0, 2, part).start()

    def pair(step, carry):
        order = 2 * step
        factor_of = jnp.where(step == 0, 0.5, 1.0)
        for chain in range(CHAINS):
            middle(chain, axis_of(chain, 0), order)
        for chain in range(CHAINS):
            advance(chain, axis_of(chain, 0), order, factor_of)
            multiply(chain, axis_of(chain, 1), order + 1)
        for chain in range(CHAINS):
            settle(chain, axis_of(chain, 0), order)
        for chain in range(CHAINS):
            middle(chain, axis_of(chain, 1), order + 1)

        if isinstance(step, int):
            return carry
        for chain in range(CHAINS):
            advance(chain, axis_of(chain, 1), order + 1, 1.0)
            multiply(chain, axis_of(chain, 0), order + 2)
        for chain in range(CHAINS):
            settle(chain, axis_of(chain, 1), order + 1)
        return carry

    lax.fori_loop(0, DEGREE // 2 - 1, pair, 0)
    pair(DEGREE // 2 - 1, 0)
    for chain in range(CHAINS):
        advance(chain, axis_of(chain, 1), DEGREE - 1, 1.0)
        start[rows_of(chain)] = vectors[chain, axis_of(chain, 1), :, slot(0)]

    hk = k_all // 2

    def small_copy(which, stage, part, k):
        axis = (part + stage) % 2
        return remote(
            small_out.at[which, stage, pl.ds(part * hk, hk)], small_in.at[which, stage, k, pl.ds(part * hk, hk)],
            small_send.at[which, stage, part, k], small_recv.at[which, stage, part, k], axis, k,
        )

    def small_start(which, stage):
        for k in (2, 1, 3):
            for part in (0, 1):
                small_copy(which, stage, part, k).start()

    def small_sum(which, stage):
        for k in (1, 3, 2):
            for part in (0, 1):
                small_copy(which, stage, part, k).wait_recv()
        return (small_out[which, stage] + small_in[which, stage, 1]) + (small_in[which, stage, 2] + small_in[which, stage, 3])

    filtered = start[...]
    small_out[0, 0] = exact_dot(filtered, filtered, NT)
    small_start(0, 0)
    for chain in range(CHAINS):
        multiply(chain, FIRST[chain], None)
    for chain in range(CHAINS):
        settle(chain, axis_of(chain, 1), DEGREE - 1)
    small_out[0, 1] = small_sum(0, 0)
    small_start(0, 1)
    for chain in range(CHAINS):
        for k in (1, 3, 2):
            last_copy(chain, k).wait_recv()
        product = (partial[chain, FIRST[chain], :, slot(0)] + last_in[chain, 1]) + (last_in[chain, 2] + last_in[chain, 3])
        image_own[rows_of(chain)] = product
    image = image_own[...] * (0.5 * radius) + centre * filtered
    small_out[1, 0] = exact_dot(filtered * DOWN, image * DOWN, NT)
    small_start(1, 0)
    gram = small_sum(0, 1)

    row_at = lax.broadcasted_iota(jnp.int32, (k_all, k_all), 0)
    column_at = lax.broadcasted_iota(jnp.int32, (k_all, k_all), 1)

    work[:, pl.ds(0, k_all)] = gram
    work[:, pl.ds(k_all, k_all)] = jnp.where(row_at == column_at, 1.0, 0.0)
    panel_row = lax.broadcasted_iota(jnp.int32, (PANEL, k_all), 0)

    def eliminate(panel):
        rows = pl.ds(panel * PANEL, PANEL)
        left, right = work[rows, pl.ds(0, k_all)], work[rows, pl.ds(k_all, k_all)]
        for group in range(0, PANEL, GROUP):
            at = panel * PANEL + group
            spread = [jnp.broadcast_to(left[:, at + t : at + t + 1], (PANEL, k_all)) for t in range(GROUP)]
            for t in range(GROUP):
                j = group + t
                inverse = lax.rsqrt(spread[t][j : j + 1, :])
                multiplier = jnp.where(panel_row > j, spread[t], 0.0) * inverse
                for later in range(t + 1, GROUP):
                    spread[later] = spread[later] - multiplier * (spread[later][j : j + 1, :] * inverse)
                left_row, right_row = left[j : j + 1, :] * inverse, right[j : j + 1, :] * inverse
                left = jnp.where(panel_row == j, left_row, left - multiplier * left_row)
                right = jnp.where(panel_row == j, right_row, right - multiplier * right_row)
        work[rows, pl.ds(0, k_all)] = left
        work[rows, pl.ds(k_all, k_all)] = right
        done = (panel + 1) * PANEL
        if done < k_all:
            below = pl.ds(done, k_all - done)
            work[below, :] = work[below, :] - exact_dot(left[:, done:k_all], work[rows, :], TN)

    panels = k_all // PANEL
    for panel in range(panels // 2):
        eliminate(panel)
    small_out[1, 1] = small_sum(1, 0)
    small_start(1, 1)
    for panel in range(panels // 2, panels):
        eliminate(panel)
    inverse_low = work[:, pl.ds(k_all, k_all)]
    basis = exact_dot(inverse_low, filtered, NN)
    mapped = exact_dot(inverse_low, image, NN)
    basis_out[...] = basis.T
    inner = small_sum(1, 1)
    projected = exact_dot(exact_dot(inverse_low / DOWN, inner, NN), inverse_low / DOWN, NT)
    projected_out[...] = projected
    residual_out[...] = (mapped - exact_dot(projected, basis, TN)).T

    for (ky, kx), axis in block_copies:
        block_copy(ky, kx, axis).wait_send()
    top_copy.wait_send()
    side_copy.wait_send()
    for chain in range(CHAINS):
        for k in (1, 2, 3):
            last_copy(chain, k).wait_send()
    for which in (0, 1):
        for stage in (0, 1):
            for part in (0, 1):
                for k in (1, 2, 3):
                    small_copy(which, stage, part, k).wait_send()


def local(factor, initial, bounds):
    nb, k_all = initial.shape
    kc = k_all // CHAINS
    vmem = pl.BlockSpec(memory_space=pltpu.VMEM)
    hbm = pl.BlockSpec(memory_space=pltpu.HBM)
    dma = pltpu.SemaphoreType.DMA
    long = SIDE * nb
    return pl.pallas_call(
        kernel,
        out_shape=(
            jax.ShapeDtypeStruct((nb, k_all), F32),
            jax.ShapeDtypeStruct((k_all, k_all), F32),
            jax.ShapeDtypeStruct((nb, k_all), F32),
        ),
        in_specs=[hbm, hbm, pl.BlockSpec(memory_space=pltpu.SMEM)],
        out_specs=(vmem, vmem, vmem),
        scratch_shapes=[
            pltpu.VMEM((len(LOCAL), nb, nb), F32),
            pltpu.VMEM((SIDE, SIDE, nb, nb), F32),
            pltpu.VMEM((nb, nb // 2), F32),
            pltpu.VMEM((k_all, nb), F32),
            pltpu.VMEM((2, SIDE, long, nb), BF16),
            pltpu.VMEM((2, SIDE, long, nb), BF16),
            pltpu.VMEM((CHAINS, 2, kc, long), F32),
            pltpu.VMEM((CHAINS, 2 * kc, long), BF16),
            pltpu.VMEM((CHAINS, 2, kc, long), F32),
            pltpu.VMEM((CHAINS, 2, kc, long), F32),
            pltpu.VMEM((4, CHAINS, kc, long), F32),
            pltpu.VMEM((4, CHAINS, kc, long), F32),
            pltpu.VMEM((CHAINS, SIDE, kc, nb), F32),
            pltpu.VMEM((k_all, nb), F32),
            pltpu.VMEM((2, 2, k_all, k_all), F32),
            pltpu.VMEM((2, 2, SIDE, k_all, k_all), F32),
            pltpu.VMEM((k_all, 2 * k_all), F32),
            pltpu.VMEM((nb, k_all), F32),
            dma((len(LOCAL) + 1,)),
            dma((SIDE, SIDE)),
            dma((SIDE, SIDE)),
            dma((4, CHAINS, 4, 2)),
            dma((4, CHAINS, 4, 2)),
            dma((2, CHAINS, SIDE)),
            dma((2, CHAINS, SIDE)),
            dma((2, 2, 2, SIDE)),
            dma((2, 2, 2, SIDE)),
        ],
        compiler_params=pltpu.CompilerParams(collective_id=0, has_side_effects=True, vmem_limit_bytes=52 << 20),
    )(factor, initial, bounds)


def solution(mesh):
    in_specs = (P(("bulk", "blk"), None), P(("bulk", "blk"), None), P("bulk"))
    out_specs = (P(("bulk", "blk"), None), P("bulk", None), P(("bulk", "blk"), None))
    return jax.shard_map(local, mesh=mesh, in_specs=in_specs, out_specs=out_specs, check_vma=False)
```

```python
import functools

import jax
import jax.numpy as jnp
from jax import lax
from jax.experimental import pallas as pl
from jax.experimental.pallas import tpu as pltpu
from jax.sharding import PartitionSpec as P

DEGREE = 8
SIDE = 4
CHAINS = 4
PANEL = 32
GROUP = 16
DOWN = 2.0**-12
X, Y = 0, 1
FIRST = (X, Y, X, Y)
MESH = pl.DeviceIdType.MESH
F32, BF16 = jnp.float32, jnp.bfloat16
HIGHEST = lax.Precision.HIGHEST
NN = (((1,), (0,)), ((), ()))
NT = (((1,), (1,)), ((), ()))
TN = (((0,), (0,)), ((), ()))

OVER_X = ((1, 1), (3, 3), (2, 1), (2, 3))
OVER_Y = ((1, 3), (3, 1), (1, 2), (3, 2))
LOCAL = ((0, 0), (1, 0), (2, 0), (3, 0), (0, 1), (0, 2), (0, 3))


def exact_dot(left, right, dims):
    return lax.dot_general(left, right, dims, precision=HIGHEST, preferred_element_type=F32)


def xor(value, k):
    if k == 0:
        return value
    if k == 1:
        return value + 1 - 2 * (value % 2)
    if k == 2:
        return (value + 2) % 4
    return 3 - value


def split(value):
    high = value.astype(BF16)
    low = (value - high.astype(F32)).astype(BF16)
    return high, low


def kernel(
    factor, initial, bounds,
    basis_out, projected_out, residual_out,
    own_blocks, arrived, arrived_half, start, w_high, w_low, vectors, stacked, partial, sums, from_first, from_second,
    last_in, image_own, small_out, small_in, work, staged,
    own_sem, block_send, block_recv, x_send, x_recv, last_send, last_recv, small_send, small_recv,
):
    me = lax.axis_index("blk")
    my_y, my_x = me // SIDE, me % SIDE
    nb, k_all = start.shape[1], start.shape[0]
    kc = k_all // CHAINS
    hc = kc // 2
    half = nb // 2

    def peer(axis, k):
        if axis == X:
            return {"blk": my_y * SIDE + xor(my_x, k)}
        return {"blk": xor(my_y, k) * SIDE + my_x}

    def column(ky, kx):
        return pl.multiple_of((xor(my_y, ky) * SIDE + xor(my_x, kx)) * nb, nb)

    def remote(src, dst, send, recv, axis, k):
        return pltpu.make_async_remote_copy(
            src_ref=src, dst_ref=dst, send_sem=send, recv_sem=recv, device_id=peer(axis, k), device_id_type=MESH
        )

    def own_copy(at):
        ky, kx = LOCAL[at]
        return pltpu.make_async_copy(factor.at[:, pl.ds(column(ky, kx), nb)], own_blocks.at[at], own_sem.at[at])

    barrier = pltpu.get_barrier_semaphore()
    for axis in (X, Y):
        for k in (1, 2, 3):
            pl.semaphore_signal(barrier, inc=1, device_id=peer(axis, k), device_id_type=MESH)

    initial_copy = pltpu.make_async_copy(initial, staged, own_sem.at[len(LOCAL)])
    initial_copy.start()
    for at in range(len(LOCAL)):
        own_copy(at).start()

    low_end, high_end = bounds[0], bounds[1]
    centre = (low_end + high_end) / 2.0
    radius = (high_end - low_end) / 2.0
    scale = 2.0 / radius

    def put(axis, k_out, k_in, rows, columns, value):
        high, low = split(value)
        w_high[axis, k_out, pl.ds(k_in * nb + rows[0], rows[1]), pl.ds(columns[0], columns[1])] = high
        w_low[axis, k_out, pl.ds(k_in * nb + rows[0], rows[1]), pl.ds(columns[0], columns[1])] = low

    whole = (0, nb)

    def place(ky, kx, value, axis):
        value = value * scale
        if axis == X:
            put(Y, ky, kx, whole, whole, value)
            put(X, kx, ky, whole, whole, value.T)
        else:
            put(X, kx, ky, whole, whole, value)
            put(Y, ky, kx, whole, whole, value.T)

    initial_copy.wait()
    start[...] = staged[...].T
    for chain in range(CHAINS):
        vectors[chain, FIRST[chain]] = jnp.zeros((kc, SIDE * nb), F32)

    pl.semaphore_wait(barrier, 6)

    def rows_of(chain):
        return pl.ds(chain * kc, kc)

    def slot(k):
        return pl.ds(k * nb, nb)

    def first_copy(chain, k):
        axis = 1 - FIRST[chain]
        return remote(
            start.at[rows_of(chain)], vectors.at[chain, axis, :, slot(k)],
            last_send.at[0, chain, k], last_recv.at[0, chain, k], axis, k,
        )

    def last_copy(chain, k):
        axis = FIRST[chain]
        return remote(
            partial.at[chain, axis, :, slot(k)], last_in.at[chain, k],
            last_send.at[1, chain, k], last_recv.at[1, chain, k], axis, k,
        )

    def block_copy(ky, kx, axis):
        return remote(
            factor.at[:, pl.ds(column(ky, kx), nb)], arrived.at[ky, kx],
            block_send.at[ky, kx], block_recv.at[ky, kx], axis, kx if axis == X else ky,
        )

    top_copy = remote(
        factor.at[pl.ds(0, half), pl.ds(column(2, 2), nb)], arrived.at[2, 2, pl.ds(0, half)],
        block_send.at[2, 2], block_recv.at[2, 2], X, 2,
    )
    side_copy = remote(
        factor.at[:, pl.ds(pl.multiple_of(column(2, 2) + half, half), half)], arrived_half,
        block_send.at[0, 0], block_recv.at[0, 0], Y, 2,
    )

    for chain in range(CHAINS):
        for k in (2, 1, 3):
            first_copy(chain, k).start()
    block_copies = []
    for over_x, over_y in zip(OVER_X, OVER_Y):
        block_copies += [(over_x, X), (over_y, Y)]
    for (ky, kx), axis in block_copies:
        block_copy(ky, kx, axis).start()
    top_copy.start()
    side_copy.start()

    for at, (ky, kx) in enumerate(LOCAL):
        own_copy(at).wait()
        value = own_blocks[at]
        if at == 0:
            row_at = lax.broadcasted_iota(jnp.int32, (nb, nb), 0)
            column_at = lax.broadcasted_iota(jnp.int32, (nb, nb), 1)
            value = jnp.where(row_at == column_at, value - centre, value)
        place(ky, kx, value, X if kx == 0 else Y)

    def stack(chain, k, value):
        high, low = split(value)
        stacked[chain, pl.ds(0, kc), slot(k)] = high
        stacked[chain, pl.ds(kc, kc), slot(k)] = low

    for chain in range(CHAINS):
        axis = 1 - FIRST[chain]
        vectors[chain, axis, :, slot(0)] = start[rows_of(chain)]
        for k in (1, 3, 2):
            first_copy(chain, k).wait()
        for k in range(SIDE):
            stack(chain, k, vectors[chain, axis, :, slot(k)])
    def parts():
        return ((0, 1, 3), (1, 3, 1))

    def exchange(chain, axis, order, stage, part):
        which, first, second = parts()[part]
        rows = pl.ds(which * hc, hc)
        lanes = pl.ds((stage // 2) * 2 * nb, 2 * nb)
        source = (partial, sums)[stage % 2].at[chain, axis, rows, lanes]
        target = (from_first, from_second)[stage % 2].at[order % 4, chain, rows, lanes]
        return remote(
            source, target, x_send.at[order % 4, chain, stage, part], x_recv.at[order % 4, chain, stage, part],
            axis, (first, second)[stage % 2],
        )

    def dots(chain, axis, slots):
        for k in slots:
            both = lax.dot_general(stacked[chain], w_high[axis, k], NN, preferred_element_type=F32)
            rest = lax.dot_general(stacked[chain, pl.ds(0, kc)], w_low[axis, k], NN, preferred_element_type=F32)
            partial[chain, axis, :, slot(k)] = both[:kc] + (both[kc:] + rest)

    def multiply(chain, axis, send):
        if send is None:
            for k in (2, 1, 3, 0):
                dots(chain, axis, (k,))
                if k:
                    last_copy(chain, k).start()
        else:
            for piece in (0, 2):
                dots(chain, axis, (piece, piece + 1))
                for part in (0, 1):
                    exchange(chain, axis, send, piece, part).start()

    def middle(chain, axis, order):
        for piece in (0, 1):
            for part, (which, first, _) in enumerate(parts()):
                rows = pl.ds(which * hc, hc)
                exchange(chain, axis, order, 2 * piece, part).wait_recv()
                mine = piece if first == 1 else 1 - piece
                for k in (2 * mine, 2 * mine + 1):
                    sums[chain, axis, rows, slot(k)] = (
                        partial[chain, axis, rows, slot(k)] + from_first[order % 4, chain, rows, slot(k ^ first)]
                    )
                exchange(chain, axis, order, 2 * mine + 1, part).start()

    def advance(chain, axis, order, factor_of):
        for piece in (0, 1):
            for part, (which, _, second) in enumerate(parts()):
                rows = pl.ds(which * hc, hc)
                mine = piece if second == 1 else 1 - piece
                exchange(chain, axis, order, 2 * piece + 1, part).wait_recv()
                for k in (2 * mine, 2 * mine + 1):
                    product = sums[chain, axis, rows, slot(k)] + from_second[order % 4, chain, rows, slot(k ^ second)]
                    value = factor_of * product - vectors[chain, axis, rows, slot(k)]
                    vectors[chain, axis, rows, slot(k)] = value
                    high, low = split(value)
                    stacked[chain, rows, slot(k)] = high
                    stacked[chain, pl.ds(kc + which * hc, hc), slot(k)] = low

    def settle(chain, axis, order):
        for stage in range(4):
            for part in (0, 1):
                exchange(chain, axis, order, stage, part).wait_send()

    def axis_of(chain, later):
        return (FIRST[chain] + later) % 2

    for (ky, kx), axis in block_copies:
        block_copy(ky, kx, axis).wait_recv()
        place(ky, kx, arrived[ky, kx], axis)
    for chain in range(CHAINS):
        dots(chain, FIRST[chain], (0, 1, 3))
    top_copy.wait_recv()
    top = arrived[2, 2, pl.ds(0, half)] * scale
    put(Y, 2, 2, (0, half), whole, top)
    put(X, 2, 2, whole, (0, half), top.T)
    side_copy.wait_recv()
    side = arrived_half[...] * scale
    put(X, 2, 2, whole, (half, half), side)
    put(Y, 2, 2, (half, half), whole, side.T)

    for chain in range(CHAINS):
        dots(chain, FIRST[chain], (2,))
        for part in (0, 1):
            exchange(chain, FIRST[chain], 0, 0, part).start()
            exchange(chain, FIRST[chain], 0, 2, part).start()

    def pair(step, carry):
        order = 2 * step
        factor_of = jnp.where(step == 0, 0.5, 1.0)
        for chain in range(CHAINS):
            middle(chain, axis_of(chain, 0), order)
        for chain in range(CHAINS):
            advance(chain, axis_of(chain, 0), order, factor_of)
            multiply(chain, axis_of(chain, 1), order + 1)
        for chain in range(CHAINS):
            settle(chain, axis_of(chain, 0), order)
        for chain in range(CHAINS):
            middle(chain, axis_of(chain, 1), order + 1)

        if isinstance(step, int):
            return carry
        for chain in range(CHAINS):
            advance(chain, axis_of(chain, 1), order + 1, 1.0)
            multiply(chain, axis_of(chain, 0), order + 2)
        for chain in range(CHAINS):
            settle(chain, axis_of(chain, 1), order + 1)
        return carry

    lax.fori_loop(0, DEGREE // 2 - 1, pair, 0)
    pair(DEGREE // 2 - 1, 0)
    for chain in range(CHAINS):
        advance(chain, axis_of(chain, 1), DEGREE - 1, 1.0)
        start[rows_of(chain)] = vectors[chain, axis_of(chain, 1), :, slot(0)]

    hk = k_all // 2

    def small_copy(which, stage, part, k):
        axis = (part + stage) % 2
        return remote(
            small_out.at[which, stage, pl.ds(part * hk, hk)], small_in.at[which, stage, k, pl.ds(part * hk, hk)],
            small_send.at[which, stage, part, k], small_recv.at[which, stage, part, k], axis, k,
        )

    def small_start(which, stage):
        for k in (2, 1, 3):
            for part in (0, 1):
                small_copy(which, stage, part, k).start()

    def small_sum(which, stage):
        for k in (1, 3, 2):
            for part in (0, 1):
                small_copy(which, stage, part, k).wait_recv()
        return (small_out[which, stage] + small_in[which, stage, 1]) + (small_in[which, stage, 2] + small_in[which, stage, 3])

    filtered = start[...]
    small_out[0, 0] = exact_dot(filtered, filtered, NT)
    small_start(0, 0)
    for chain in range(CHAINS):
        multiply(chain, FIRST[chain], None)
    for chain in range(CHAINS):
        settle(chain, axis_of(chain, 1), DEGREE - 1)
    small_out[0, 1] = small_sum(0, 0)
    small_start(0, 1)
    for chain in range(CHAINS):
        for k in (1, 3, 2):
            last_copy(chain, k).wait_recv()
        product = (partial[chain, FIRST[chain], :, slot(0)] + last_in[chain, 1]) + (last_in[chain, 2] + last_in[chain, 3])
        image_own[rows_of(chain)] = product
    image = image_own[...] * (0.5 * radius) + centre * filtered
    small_out[1, 0] = exact_dot(filtered * DOWN, image * DOWN, NT)
    small_start(1, 0)
    gram = small_sum(0, 1)

    row_at = lax.broadcasted_iota(jnp.int32, (k_all, k_all), 0)
    column_at = lax.broadcasted_iota(jnp.int32, (k_all, k_all), 1)

    work[:, pl.ds(0, k_all)] = gram
    work[:, pl.ds(k_all, k_all)] = jnp.where(row_at == column_at, 1.0, 0.0)
    panel_row = lax.broadcasted_iota(jnp.int32, (PANEL, k_all), 0)

    def eliminate(panel):
        rows = pl.ds(panel * PANEL, PANEL)
        left, right = work[rows, pl.ds(0, k_all)], work[rows, pl.ds(k_all, k_all)]
        for group in range(0, PANEL, GROUP):
            at = panel * PANEL + group
            spread = [jnp.broadcast_to(left[:, at + t : at + t + 1], (PANEL, k_all)) for t in range(GROUP)]
            for t in range(GROUP):
                j = group + t
                inverse = lax.rsqrt(spread[t][j : j + 1, :])
                multiplier = jnp.where(panel_row > j, spread[t], 0.0) * inverse
                for later in range(t + 1, GROUP):
                    spread[later] = spread[later] - multiplier * (spread[later][j : j + 1, :] * inverse)
                left_row, right_row = left[j : j + 1, :] * inverse, right[j : j + 1, :] * inverse
                left = jnp.where(panel_row == j, left_row, left - multiplier * left_row)
                right = jnp.where(panel_row == j, right_row, right - multiplier * right_row)
        work[rows, pl.ds(0, k_all)] = left
        work[rows, pl.ds(k_all, k_all)] = right
        done = (panel + 1) * PANEL
        if done < k_all:
            below = pl.ds(done, k_all - done)
            work[below, :] = work[below, :] - exact_dot(left[:, done:k_all], work[rows, :], TN)

    panels = k_all // PANEL
    for panel in range(panels // 2):
        eliminate(panel)
    small_out[1, 1] = small_sum(1, 0)
    small_start(1, 1)
    for panel in range(panels // 2, panels):
        eliminate(panel)
    inverse_low = work[:, pl.ds(k_all, k_all)]
    basis = exact_dot(inverse_low, filtered, NN)
    mapped = exact_dot(inverse_low, image, NN)
    basis_out[...] = basis.T
    inner = small_sum(1, 1)
    projected = exact_dot(exact_dot(inverse_low / DOWN, inner, NN), inverse_low / DOWN, NT)
    projected_out[...] = projected
    residual_out[...] = (mapped - exact_dot(projected, basis, TN)).T

    for (ky, kx), axis in block_copies:
        block_copy(ky, kx, axis).wait_send()
    top_copy.wait_send()
    side_copy.wait_send()
    for chain in range(CHAINS):
        for k in (1, 2, 3):
            last_copy(chain, k).wait_send()
    for which in (0, 1):
        for stage in (0, 1):
            for part in (0, 1):
                for k in (1, 2, 3):
                    small_copy(which, stage, part, k).wait_send()


def local(factor, initial, bounds):
    nb, k_all = initial.shape
    kc = k_all // CHAINS
    vmem = pl.BlockSpec(memory_space=pltpu.VMEM)
    hbm = pl.BlockSpec(memory_space=pltpu.HBM)
    dma = pltpu.SemaphoreType.DMA
    long = SIDE * nb
    return pl.pallas_call(
        kernel,
        out_shape=(
            jax.ShapeDtypeStruct((nb, k_all), F32),
            jax.ShapeDtypeStruct((k_all, k_all), F32),
            jax.ShapeDtypeStruct((nb, k_all), F32),
        ),
        in_specs=[hbm, hbm, pl.BlockSpec(memory_space=pltpu.SMEM)],
        out_specs=(vmem, vmem, vmem),
        scratch_shapes=[
            pltpu.VMEM((len(LOCAL), nb, nb), F32),
            pltpu.VMEM((SIDE, SIDE, nb, nb), F32),
            pltpu.VMEM((nb, nb // 2), F32),
            pltpu.VMEM((k_all, nb), F32),
            pltpu.VMEM((2, SIDE, long, nb), BF16),
            pltpu.VMEM((2, SIDE, long, nb), BF16),
            pltpu.VMEM((CHAINS, 2, kc, long), F32),
            pltpu.VMEM((CHAINS, 2 * kc, long), BF16),
            pltpu.VMEM((CHAINS, 2, kc, long), F32),
            pltpu.VMEM((CHAINS, 2, kc, long), F32),
            pltpu.VMEM((4, CHAINS, kc, long), F32),
            pltpu.VMEM((4, CHAINS, kc, long), F32),
            pltpu.VMEM((CHAINS, SIDE, kc, nb), F32),
            pltpu.VMEM((k_all, nb), F32),
            pltpu.VMEM((2, 2, k_all, k_all), F32),
            pltpu.VMEM((2, 2, SIDE, k_all, k_all), F32),
            pltpu.VMEM((k_all, 2 * k_all), F32),
            pltpu.VMEM((nb, k_all), F32),
            dma((len(LOCAL) + 1,)),
            dma((SIDE, SIDE)),
            dma((SIDE, SIDE)),
            dma((4, CHAINS, 4, 2)),
            dma((4, CHAINS, 4, 2)),
            dma((2, CHAINS, SIDE)),
            dma((2, CHAINS, SIDE)),
            dma((2, 2, 2, SIDE)),
            dma((2, 2, 2, SIDE)),
        ],
        compiler_params=pltpu.CompilerParams(collective_id=0, has_side_effects=True, vmem_limit_bytes=52 << 20),
    )(factor, initial, bounds)


def solution(mesh):
    in_specs = (P(("bulk", "blk"), None), P(("bulk", "blk"), None), P("bulk"))
    out_specs = (P(("bulk", "blk"), None), P("bulk", None), P(("bulk", "blk"), None))
    return jax.shard_map(local, mesh=mesh, in_specs=in_specs, out_specs=out_specs, check_vma=False)
```
